256 devices in a mesh: row: 32 (over z, y_hi, core), off: 8 (over x, y_lo).
Axes of the slice: x: 4, y: 4 (y_hi: 2, y_lo: 2; y = y_hi * 2 + y_lo), z: 8, core: 2. Of those that a mesh axis runs over, the one named last changes fastest.
Arguments:
- vectors: float32 [32768, 128], P(('row', 'off')), may hold values from -6 to 6
- blocks: float32 [32, 8, 48, 128, 128], P('row', 'off'), may hold values from -0.0546875 to 0.0546875
- lists: int32 [32, 8, 2, 48], P('row', 'off'), may hold values from 0 to 7, as said below
Outputs:
- filtered: float32 [32768, 128], P(('row', 'off'))
The draws below stay inside these ranges and needn't reach their ends.
Inputs may be any that keep to these rules, and one draw needn't show every extreme that they name: `lists`: within each tile the 48 listed blocks are distinct positions of its 8 x 8 grid of blocks.
All inputs are finite; a program needn't handle non-finite values.
Results may differ from the reference program's by a relative error of at most 0.00011.
Values sent between devices are 32-bit elements; how exact they have to be, the bound alone decides.
A program may use at most 64 MiB of HBM per device.

```python
import jax
import jax.numpy as jnp
from jax import lax

TILE = 1024
BS = 128
NV = 128
DEGREE = 4
TB = 8
NBLK = 48
ROW_BLOCKS = 32
OFFSETS = 8
STATES = 32768
N_OFF = 8


def draw_lists(key, part):
    key_list = jax.random.split(jax.random.fold_in(key, 17), ROW_BLOCKS * OFFSETS)

    def one_tile(tile_key):
        return jax.random.permutation(tile_key, TB * TB)[:NBLK]
    chosen = jax.vmap(one_tile)(key_list).astype(jnp.int32)
    chosen = chosen.reshape(ROW_BLOCKS, OFFSETS, NBLK)
    return jnp.stack([chosen // TB, chosen % TB], axis=2).astype(jnp.int32)


def block_scale(key, extent, pieces, least, top_value):
    gain, own = 1.0, jax.random.fold_in(key, 6)
    for dim, blocks in pieces:
        heights = jnp.exp(jax.random.uniform(jax.random.fold_in(own, dim), (blocks,), jnp.float32, least / len(pieces), top_value / len(pieces)))
        gain = gain * jnp.repeat(heights, extent[dim] // blocks).reshape([-1 if axis == dim else 1 for axis in range(len(extent))])
    return gain


def bell_draw(stream_key, extent, spread, bound, cuts=(), kind=jnp.bfloat16):
    result = jax.random.normal(stream_key, extent, jnp.float32) * spread
    if len(cuts) > 0:
        result = block_scale(stream_key, extent, cuts, -0.22, 0.18) * result
    return jnp.clip(result, min=-bound, max=bound).astype(kind)


def setup_inputs(seed: int = 0) -> dict:
    splits = jax.random.split(jax.random.key(seed), 4)
    vectors = bell_draw(splits[0], (STATES, NV), 1.0, 6.0, ((0, 256),), jnp.float32)
    blocks = bell_draw(splits[1], (ROW_BLOCKS, OFFSETS, NBLK, BS, BS), (NBLK * BS * (2 * N_OFF - 1) // TB) ** -0.5, 0.0546875, ((0, 32), (1, 8)), jnp.float32)
    lists = draw_lists(jax.random.fold_in(splits[3], 71), 0)
    return {"vectors": vectors, "blocks": blocks, "lists": lists}


first_scale = 0.4
later_scale = 0.8


def apply_hamiltonian(field, blocks, lists):
    shaped = field.reshape(ROW_BLOCKS, TB, BS, NV)
    offset_range = jnp.arange(OFFSETS, dtype=jnp.int32)

    def one_row(block_row, totals):
        stored = blocks[block_row]
        row_list = lists[block_row, :, 0, :]
        col_list = lists[block_row, :, 1, :]
        far_rows = ((block_row + offset_range) % ROW_BLOCKS).astype(jnp.int32)
        far_vectors = shaped[far_rows[:, None], col_list]
        own_vectors = shaped[block_row, row_list]
        direct = jnp.einsum("okab,okbv->okav", stored, far_vectors, precision=lax.Precision.HIGHEST)
        transposed = jnp.einsum("okab,okav->okbv", stored, own_vectors, precision=lax.Precision.HIGHEST)
        totals = totals.at[block_row, row_list].add(direct)
        totals = totals.at[far_rows[:, None], col_list].add(transposed)
        return totals

    totals = lax.fori_loop(0, ROW_BLOCKS, one_row, jnp.zeros((ROW_BLOCKS, TB, BS, NV), jnp.float32))
    return totals.reshape(ROW_BLOCKS * TILE, NV)


def reference(vectors, blocks, lists):
    previous = vectors
    current = first_scale * apply_hamiltonian(vectors, blocks, lists)
    for degree in range(1, DEGREE):
        following = later_scale * apply_hamiltonian(current, blocks, lists) - previous
        previous, current = current, following
    return current
```

```python
import functools

import jax
import jax.numpy as jnp
from jax import lax
from jax.experimental import pallas as pl
from jax.experimental.pallas import tpu as pltpu
from jax.sharding import PartitionSpec as P

DEGREE = 4
MESH = pl.DeviceIdType.MESH

first_scale = 0.4
later_scale = 0.8


def split(x):
    hi = x.astype(jnp.bfloat16)
    lo = (x - hi.astype(jnp.float32)).astype(jnp.bfloat16)
    return hi, lo


def kernel(
    n_row, n_off, bs, chunk,
    where_ref, vec_ref, blocks_hbm, out_ref,
    blocks, a_hi, a_lo, t_hi, t_lo, cur, near, far, xb, ahead, back, got_ahead, got_back,
    load_sem, near_send, far_send, near_recv, far_recv, ahead_send, back_send, ahead_recv, back_recv,
):
    row = lax.axis_index("row")
    off = lax.axis_index("off")
    rows = n_off * bs
    per_chunk = chunk // bs

    def at_row(r):
        return lax.rem(r + n_row, n_row)

    load = pltpu.make_async_copy(blocks_hbm, blocks, load_sem)
    load.start()

    barrier = pltpu.get_barrier_semaphore()
    for s in range(1, n_off):
        pl.semaphore_signal(
            barrier, inc=1, device_id=(row, lax.rem(off + s, n_off)), device_id_type=MESH
        )
        pl.semaphore_signal(barrier, inc=1, device_id=(at_row(row - s), s), device_id_type=MESH)

    @pl.when(off > 0)
    def _():
        for t in range(n_off):
            pl.semaphore_signal(
                barrier, inc=1, device_id=(at_row(row + off), t), device_id_type=MESH
            )

    cur[0] = vec_ref[...]
    cur[1] = jnp.zeros_like(cur[1])

    @pl.when(off > 0)
    def _():
        pl.semaphore_wait(barrier, 3 * n_off - 2)

    @pl.when(off == 0)
    def _():
        pl.semaphore_wait(barrier, 2 * n_off - 2)

    def near_copy(par, s):
        return pltpu.make_async_remote_copy(
            src_ref=cur.at[par],
            dst_ref=near.at[par, off],
            send_sem=near_send.at[s],
            recv_sem=near_recv.at[par, off],
            device_id=(row, lax.rem(off + s, n_off)),
            device_id_type=MESH,
        )

    def far_copy(par, s):
        return pltpu.make_async_remote_copy(
            src_ref=cur.at[par],
            dst_ref=far.at[par, off],
            send_sem=far_send.at[s],
            recv_sem=far_recv.at[par, off],
            device_id=(at_row(row - s), s),
            device_id_type=MESH,
        )

    def send_piece(par):
        for s in range(1, n_off):
            near_copy(par, s).start()
        for s in range(n_off - 1, 0, -1):
            far_copy(par, s).start()

    def await_slot(ref, sem):
        pltpu.make_async_remote_copy(
            src_ref=ref, dst_ref=ref, send_sem=near_send.at[0], recv_sem=sem,
            device_id=(row, lax.rem(off + 1, n_off)), device_id_type=MESH,
        ).wait_recv()

    def back_copy(par, t):
        return pltpu.make_async_remote_copy(
            src_ref=back.at[t],
            dst_ref=got_back.at[par, off],
            send_sem=back_send.at[t],
            recv_sem=back_recv.at[par, off],
            device_id=(at_row(row + off), t),
            device_id_type=MESH,
        )

    def ahead_copy(par, t):
        return pltpu.make_async_remote_copy(
            src_ref=ahead.at[t],
            dst_ref=got_ahead.at[par, off],
            send_sem=ahead_send.at[t],
            recv_sem=ahead_recv.at[par, off],
            device_id=(row, t),
            device_id_type=MESH,
        )

    def wait_back(par):
        @pl.when(off > 0)
        def _():
            for t in range(n_off):
                back_copy(par, t).wait_send()

    def wait_ahead(par):
        for s in range(1, n_off):
            ahead_copy(par, lax.rem(off + s, n_off)).wait_send()

    send_piece(0)
    load.wait()

    def dense_row(r, carry):
        for c in range(n_off):
            k = where_ref[r * n_off + c]
            block = jnp.where(k > 0, blocks[jnp.maximum(k - 1, 0)], 0.0)
            hi, lo = split(block)
            at = pl.ds(pl.multiple_of(r * bs, bs), bs)
            a_hi[at, c * bs:(c + 1) * bs] = hi
            a_lo[at, c * bs:(c + 1) * bs] = lo
            hi, lo = split(block.T)
            t_hi[c * bs:(c + 1) * bs, at] = hi
            t_lo[c * bs:(c + 1) * bs, at] = lo
        return carry

    lax.fori_loop(0, n_off, dense_row, 0)

    def put(t, x):
        hi, lo = split(x)
        at = pl.ds(pl.multiple_of(t * bs, bs), bs)
        xb[at, :bs] = hi
        xb[at, bs:] = lo

    def product(hi_ref, lo_ref, at):
        both = jnp.dot(hi_ref[at, :], xb[...], preferred_element_type=jnp.float32)
        both += jnp.dot(lo_ref[at, :], xb[...], preferred_element_type=jnp.float32)
        return both[:, :bs] + both[:, bs:]

    n_chunks = rows // chunk

    def step(k, carry):
        par = lax.rem(k, 2)
        put(off, cur[par])

        def take_near(s, carry):
            j = lax.rem(off + s, n_off)
            await_slot(near.at[par, j], near_recv.at[par, j])
            put(j, near[par, j])
            return carry

        lax.fori_loop(1, n_off, take_near, 0)

        @pl.when(k > 0)
        def _():
            wait_back(par)

        def back_chunk(c, carry):
            at = pl.ds(pl.multiple_of(c * chunk, chunk), chunk)
            y = product(t_hi, t_lo, at)
            for p in range(per_chunk):
                t = c * per_chunk + p
                back[t] = y[p * bs:(p + 1) * bs]

                @pl.when(off > 0)
                def _():
                    back_copy(par, t).start()
            return carry

        lax.fori_loop(0, n_chunks, back_chunk, 0)

        @pl.when(off > 0)
        def _():
            def take_far(j, carry):
                await_slot(far.at[par, j], far_recv.at[par, j])
                put(j, far[par, j])
                return carry

            lax.fori_loop(0, n_off, take_far, 0)

        @pl.when(k > 0)
        def _():
            wait_ahead(par)

        def ahead_chunk(c, carry):
            at = pl.ds(pl.multiple_of(c * chunk, chunk), chunk)
            y = product(a_hi, a_lo, at)
            for p in range(per_chunk):
                t = c * per_chunk + p
                ahead[t] = y[p * bs:(p + 1) * bs] + jnp.where(off == 0, back[t], 0.0)

                @pl.when(t != off)
                def _():
                    ahead_copy(par, t).start()
            return carry

        lax.fori_loop(0, n_chunks, ahead_chunk, 0)

        total = ahead[off]
        for s in range(1, n_off):
            j = lax.rem(off + s, n_off)
            await_slot(got_ahead.at[par, j], ahead_recv.at[par, j])
            total += got_ahead[par, j]
        for s in range(1, n_off):
            await_slot(got_back.at[par, s], back_recv.at[par, s])
            total += got_back[par, s]
        scale = jnp.where(k == 0, first_scale, later_scale)
        nxt = lax.rem(k + 1, 2)
        cur[nxt] = scale * total - cur[nxt]

        for s in range(1, n_off):
            near_copy(par, s).wait_send()
            far_copy(par, s).wait_send()

        @pl.when(k < DEGREE - 1)
        def _():
            send_piece(nxt)

        return carry

    lax.fori_loop(0, DEGREE, step, 0)
    wait_back(0)
    wait_ahead(0)
    out_ref[...] = cur[DEGREE % 2]


def solution(mesh):
    n_row, n_off = mesh.shape["row"], mesh.shape["off"]

    def per_device(vectors, blocks, lists):
        bs, width = vectors.shape
        rows = n_off * bs
        count = blocks.shape[2]
        position = lists[0, 0, 0] * n_off + lists[0, 0, 1]
        hit = position[None, :] == jnp.arange(n_off * n_off, dtype=jnp.int32)[:, None]
        where = jnp.sum(
            jnp.where(hit, jnp.arange(1, count + 1, dtype=jnp.int32)[None, :], 0),
            axis=1, dtype=jnp.int32,
        )
        f32, bf16 = jnp.float32, jnp.bfloat16
        dma = pltpu.SemaphoreType.DMA
        return pl.pallas_call(
            functools.partial(kernel, n_row, n_off, bs, 2 * bs),
            out_shape=jax.ShapeDtypeStruct((bs, width), f32),
            in_specs=[
                pl.BlockSpec(memory_space=pltpu.SMEM),
                pl.BlockSpec(memory_space=pltpu.VMEM),
                pl.BlockSpec(memory_space=pl.ANY),
            ],
            out_specs=pl.BlockSpec(memory_space=pltpu.VMEM),
            scratch_shapes=[
                pltpu.VMEM((count, bs, bs), f32),
                pltpu.VMEM((rows, rows), bf16),
                pltpu.VMEM((rows, rows), bf16),
                pltpu.VMEM((rows, rows), bf16),
                pltpu.VMEM((rows, rows), bf16),
                pltpu.VMEM((2, bs, width), f32),
                pltpu.VMEM((2, n_off, bs, width), f32),
                pltpu.VMEM((2, n_off, bs, width), f32),
                pltpu.VMEM((rows, 2 * width), bf16),
                pltpu.VMEM((n_off, bs, width), f32),
                pltpu.VMEM((n_off, bs, width), f32),
                pltpu.VMEM((2, n_off, bs, width), f32),
                pltpu.VMEM((2, n_off, bs, width), f32),
                dma,
                dma((n_off,)),
                dma((n_off,)),
                dma((2, n_off)),
                dma((2, n_off)),
                dma((n_off,)),
                dma((n_off,)),
                dma((2, n_off)),
                dma((2, n_off)),
            ],
            compiler_params=pltpu.CompilerParams(collective_id=0, has_side_effects=True),
        )(where, vectors, blocks[0, 0])

    return jax.shard_map(
        per_device,
        mesh=mesh,
        in_specs=(
            P(("row", "off"), None),
            P("row", "off", None, None, None),
            P("row", "off", None, None),
        ),
        out_specs=P(("row", "off"), None),
        check_vma=False,
    )
```

```python
import functools

import jax
import jax.numpy as jnp
from jax import lax
from jax.experimental import pallas as pl
from jax.experimental.pallas import tpu as pltpu
from jax.sharding import PartitionSpec as P

DEGREE = 4
CHAINS = 2
MESH = pl.DeviceIdType.MESH

first_scale = 0.4
later_scale = 0.8


def split(x):
    hi = x.astype(jnp.bfloat16)
    lo = (x - hi.astype(jnp.float32)).astype(jnp.bfloat16)
    return hi, lo


def swap_halves(x):
    return pltpu.roll(x, x.shape[1] // 2, 1)


def left_of(shape):
    return lax.broadcasted_iota(jnp.int32, shape, 1) < shape[1] // 2


def kernel(
    n_row, n_off, bs, chunk,
    where_ref, vec_ref, blocks_hbm, out_ref,
    blocks, a_hi, a_lo, t_hi, t_lo, cur, near, far, xb, ahead, back, got_ahead, got_back,
    load_sem, near_send, far_send, near_recv, far_recv, ahead_send, back_send, ahead_recv, back_recv,
):
    row = lax.axis_index("row")
    off = lax.axis_index("off")
    rows = n_off * bs
    half = bs // 2
    per_chunk = chunk // bs
    n_chunks = rows // chunk
    left = left_of((half, bs))

    def at_row(r):
        return lax.rem(r + n_row, n_row)

    load = pltpu.make_async_copy(blocks_hbm, blocks, load_sem)
    load.start()

    barrier = pltpu.get_barrier_semaphore()
    for s in range(1, n_off):
        pl.semaphore_signal(
            barrier, inc=1, device_id=(row, lax.rem(off + s, n_off)), device_id_type=MESH
        )
        pl.semaphore_signal(barrier, inc=1, device_id=(at_row(row - s), s), device_id_type=MESH)

    @pl.when(off > 0)
    def _():
        for t in range(n_off):
            pl.semaphore_signal(
                barrier, inc=1, device_id=(at_row(row + off), t), device_id_type=MESH
            )

    upper, lower = vec_ref[:half, :], vec_ref[half:, :]
    cur[0, 0] = jnp.where(left, upper, swap_halves(lower))
    cur[1, 0] = jnp.where(left, swap_halves(upper), lower)
    for h in range(CHAINS):
        cur[h, 1] = jnp.zeros((half, bs), jnp.float32)

    @pl.when(off > 0)
    def _():
        pl.semaphore_wait(barrier, 3 * n_off - 2)

    @pl.when(off == 0)
    def _():
        pl.semaphore_wait(barrier, 2 * n_off - 2)

    def near_copy(h, par, s):
        return pltpu.make_async_remote_copy(
            src_ref=cur.at[h, par],
            dst_ref=near.at[h, par, off],
            send_sem=near_send.at[h, s],
            recv_sem=near_recv.at[h, par, off],
            device_id=(row, lax.rem(off + s, n_off)),
            device_id_type=MESH,
        )

    def far_copy(h, par, s):
        return pltpu.make_async_remote_copy(
            src_ref=cur.at[h, par],
            dst_ref=far.at[h, par, off],
            send_sem=far_send.at[h, s],
            recv_sem=far_recv.at[h, par, off],
            device_id=(at_row(row - s), s),
            device_id_type=MESH,
        )

    def back_copy(h, par, t):
        return pltpu.make_async_remote_copy(
            src_ref=back.at[h, t],
            dst_ref=got_back.at[h, par, off],
            send_sem=back_send.at[h, t],
            recv_sem=back_recv.at[h, par, off],
            device_id=(at_row(row + off), t),
            device_id_type=MESH,
        )

    def ahead_copy(h, par, t):
        return pltpu.make_async_remote_copy(
            src_ref=ahead.at[h, t],
            dst_ref=got_ahead.at[h, par, off],
            send_sem=ahead_send.at[h, t],
            recv_sem=ahead_recv.at[h, par, off],
            device_id=(row, t),
            device_id_type=MESH,
        )

    def await_slot(ref, sem):
        pltpu.make_async_remote_copy(
            src_ref=ref, dst_ref=ref, send_sem=near_send.at[0, 0], recv_sem=sem,
            device_id=(row, lax.rem(off + 1, n_off)), device_id_type=MESH,
        ).wait_recv()

    def send_piece(h, par):
        for s in range(1, n_off):
            near_copy(h, par, s).start()
        for s in range(n_off - 1, 0, -1):
            far_copy(h, par, s).start()

    def wait_back(h, par):
        @pl.when(off > 0)
        def _():
            for t in range(n_off):
                back_copy(h, par, t).wait_send()

    def wait_ahead(h, par):
        for s in range(1, n_off):
            ahead_copy(h, par, lax.rem(off + s, n_off)).wait_send()

    for h in range(CHAINS):
        send_piece(h, 0)
    load.wait()

    def dense_row(r, carry):
        for c in range(n_off):
            k = where_ref[r * n_off + c]
            block = jnp.where(k > 0, blocks[jnp.maximum(k - 1, 0)], 0.0)
            hi, lo = split(block)
            at = pl.ds(pl.multiple_of(r * bs, bs), bs)
            a_hi[at, c * bs:(c + 1) * bs] = hi
            a_lo[at, c * bs:(c + 1) * bs] = lo
            hi, lo = split(block.T)
            t_hi[c * bs:(c + 1) * bs, at] = hi
            t_lo[c * bs:(c + 1) * bs, at] = lo
        return carry

    lax.fori_loop(0, n_off, dense_row, 0)

    def put(t, x):
        hi = x.astype(jnp.bfloat16).astype(jnp.float32)
        lo = x - hi
        start = pl.multiple_of(t * bs, bs)
        xb[pl.ds(start, half), :] = jnp.where(left, hi, swap_halves(lo)).astype(jnp.bfloat16)
        xb[pl.ds(start + half, half), :] = jnp.where(left, swap_halves(hi), lo).astype(jnp.bfloat16)

    def product(hi_ref, lo_ref, at):
        both = jnp.dot(hi_ref[at, :], xb[...], preferred_element_type=jnp.float32)
        both += jnp.dot(lo_ref[at, :], xb[...], preferred_element_type=jnp.float32)
        return both + swap_halves(both)

    def packed(y, p):
        return jnp.where(left, y[p * bs:p * bs + half], y[p * bs + half:(p + 1) * bs])

    def multiply(h, par, k):
        put(off, cur[h, par])

        def take_near(s, carry):
            j = lax.rem(off + s, n_off)
            await_slot(near.at[h, par, j], near_recv.at[h, par, j])
            put(j, near[h, par, j])
            return carry

        lax.fori_loop(1, n_off, take_near, 0)

        @pl.when(k > 0)
        def _():
            wait_back(h, par)

        def back_chunk(c, carry):
            at = pl.ds(pl.multiple_of(c * chunk, chunk), chunk)
            y = product(t_hi, t_lo, at)
            for p in range(per_chunk):
                t = c * per_chunk + p
                back[h, t] = packed(y, p)

                @pl.when(off > 0)
                def _():
                    back_copy(h, par, t).start()
            return carry

        lax.fori_loop(0, n_chunks, back_chunk, 0)

        @pl.when(off > 0)
        def _():
            def take_far(j, carry):
                await_slot(far.at[h, par, j], far_recv.at[h, par, j])
                put(j, far[h, par, j])
                return carry

            lax.fori_loop(0, n_off, take_far, 0)

        @pl.when(k > 0)
        def _():
            wait_ahead(h, par)

        def ahead_chunk(c, carry):
            at = pl.ds(pl.multiple_of(c * chunk, chunk), chunk)
            y = product(a_hi, a_lo, at)
            for p in range(per_chunk):
                t = c * per_chunk + p
                ahead[h, t] = packed(y, p) + jnp.where(off == 0, back[h, t], 0.0)

                @pl.when(t != off)
                def _():
                    ahead_copy(h, par, t).start()
            return carry

        lax.fori_loop(0, n_chunks, ahead_chunk, 0)

    def collect(h, par, k):
        total = ahead[h, off]
        for s in range(1, n_off):
            j = lax.rem(off + s, n_off)
            await_slot(got_ahead.at[h, par, j], ahead_recv.at[h, par, j])
            total += got_ahead[h, par, j]
        for s in range(1, n_off):
            await_slot(got_back.at[h, par, s], back_recv.at[h, par, s])
            total += got_back[h, par, s]
        scale = jnp.where(k == 0, first_scale, later_scale)
        nxt = lax.rem(k + 1, 2)
        cur[h, nxt] = scale * total - cur[h, nxt]
        for s in range(1, n_off):
            near_copy(h, par, s).wait_send()
            far_copy(h, par, s).wait_send()

        @pl.when(k < DEGREE - 1)
        def _():
            send_piece(h, nxt)

    def step(k, carry):
        par = lax.rem(k, 2)

        def each(what):
            def one(h, carry):
                what(h, par, k)
                return carry

            lax.fori_loop(0, CHAINS, one, 0)

        each(multiply)
        each(collect)
        return carry

    lax.fori_loop(0, DEGREE, step, 0)
    last = DEGREE % 2
    for h in range(CHAINS):
        wait_back(h, 1 - last)
        wait_ahead(h, 1 - last)
    out_ref[:half, :] = jnp.where(left, cur[0, last], swap_halves(cur[1, last]))
    out_ref[half:, :] = jnp.where(left, swap_halves(cur[0, last]), cur[1, last])


def solution(mesh):
    n_row, n_off = mesh.shape["row"], mesh.shape["off"]

    def per_device(vectors, blocks, lists):
        bs, width = vectors.shape
        rows = n_off * bs
        half = bs // 2
        count = blocks.shape[2]
        position = lists[0, 0, 0] * n_off + lists[0, 0, 1]
        hit = position[None, :] == jnp.arange(n_off * n_off, dtype=jnp.int32)[:, None]
        where = jnp.sum(
            jnp.where(hit, jnp.arange(1, count + 1, dtype=jnp.int32)[None, :], 0),
            axis=1, dtype=jnp.int32,
        )
        f32, bf16 = jnp.float32, jnp.bfloat16
        dma = pltpu.SemaphoreType.DMA
        slots = pltpu.VMEM((CHAINS, 2, n_off, half, width), f32)
        staged = pltpu.VMEM((CHAINS, n_off, half, width), f32)
        return pl.pallas_call(
            functools.partial(kernel, n_row, n_off, bs, 2 * bs),
            out_shape=jax.ShapeDtypeStruct((bs, width), f32),
            in_specs=[
                pl.BlockSpec(memory_space=pltpu.SMEM),
                pl.BlockSpec(memory_space=pltpu.VMEM),
                pl.BlockSpec(memory_space=pl.ANY),
            ],
            out_specs=pl.BlockSpec(memory_space=pltpu.VMEM),
            scratch_shapes=[
                pltpu.VMEM((count, bs, bs), f32),
                pltpu.VMEM((rows, rows), bf16),
                pltpu.VMEM((rows, rows), bf16),
                pltpu.VMEM((rows, rows), bf16),
                pltpu.VMEM((rows, rows), bf16),
                pltpu.VMEM((CHAINS, 2, half, width), f32),
                slots,
                slots,
                pltpu.VMEM((rows, width), bf16),
                staged,
                staged,
                slots,
                slots,
                dma,
                dma((CHAINS, n_off)),
                dma((CHAINS, n_off)),
                dma((CHAINS, 2, n_off)),
                dma((CHAINS, 2, n_off)),
                dma((CHAINS, n_off)),
                dma((CHAINS, n_off)),
                dma((CHAINS, 2, n_off)),
                dma((CHAINS, 2, n_off)),
            ],
            compiler_params=pltpu.CompilerParams(collective_id=0, has_side_effects=True),
        )(where, vectors, blocks[0, 0])

    return jax.shard_map(
        per_device,
        mesh=mesh,
        in_specs=(
            P(("row", "off"), None),
            P("row", "off", None, None, None),
            P("row", "off", None, None),
        ),
        out_specs=P(("row", "off"), None),
        check_vma=False,
    )
```

```python
import functools

import jax
import jax.numpy as jnp
from jax import lax
from jax.experimental import pallas as pl
from jax.experimental.pallas import tpu as pltpu
from jax.sharding import PartitionSpec as P

DEGREE = 4
CHAINS = 2
MESH = pl.DeviceIdType.MESH

first_scale = 0.4
later_scale = 0.8


def split(x):
    hi = x.astype(jnp.bfloat16)
    lo = (x - hi.astype(jnp.float32)).astype(jnp.bfloat16)
    return hi, lo


def swap_halves(x):
    return pltpu.roll(x, x.shape[1] // 2, 1)


def left_of(shape):
    return lax.broadcasted_iota(jnp.int32, shape, 1) < shape[1] // 2


def kernel(
    n_row, n_off, bs, chunk,
    where_ref, vec_ref, blocks_hbm, out_ref,
    blocks, a_hi, a_lo, t_hi, t_lo, cur, near, far, xb, ahead, back, got_ahead, got_back,
    load_sem, near_send, far_send, near_recv, far_recv, ahead_send, back_send, ahead_recv, back_recv,
):
    row = lax.axis_index("row")
    off = lax.axis_index("off")
    rows = n_off * bs
    half = bs // 2
    per_chunk = chunk // bs
    n_chunks = rows // chunk
    left = left_of((half, bs))

    def at_row(r):
        return lax.rem(r + n_row, n_row)

    load = pltpu.make_async_copy(blocks_hbm, blocks, load_sem)
    load.start()

    barrier = pltpu.get_barrier_semaphore()
    for s in range(1, n_off):
        pl.semaphore_signal(
            barrier, inc=1, device_id=(row, lax.rem(off + s, n_off)), device_id_type=MESH
        )
        pl.semaphore_signal(barrier, inc=1, device_id=(at_row(row - s), s), device_id_type=MESH)

    @pl.when(off > 0)
    def _():
        for t in range(n_off):
            pl.semaphore_signal(
                barrier, inc=1, device_id=(at_row(row + off), t), device_id_type=MESH
            )

    upper, lower = vec_ref[:half, :], vec_ref[half:, :]
    cur[0, 0] = jnp.where(left, upper, swap_halves(lower))
    cur[1, 0] = jnp.where(left, swap_halves(upper), lower)
    for h in range(CHAINS):
        cur[h, 1] = jnp.zeros((half, bs), jnp.float32)

    @pl.when(off > 0)
    def _():
        pl.semaphore_wait(barrier, 3 * n_off - 2)

    @pl.when(off == 0)
    def _():
        pl.semaphore_wait(barrier, 2 * n_off - 2)

    def near_copy(h, par, s):
        return pltpu.make_async_remote_copy(
            src_ref=cur.at[h, par],
            dst_ref=near.at[h, par, off],
            send_sem=near_send.at[h, s],
            recv_sem=near_recv.at[h, par, off],
            device_id=(row, lax.rem(off + s, n_off)),
            device_id_type=MESH,
        )

    def far_copy(h, par, s):
        d = 1 + lax.rem(s + off, n_off - 1)
        return pltpu.make_async_remote_copy(
            src_ref=cur.at[h, par],
            dst_ref=far.at[h, par, off],
            send_sem=far_send.at[h, s],
            recv_sem=far_recv.at[h, par, off],
            device_id=(at_row(row - d), d),
            device_id_type=MESH,
        )

    def back_copy(h, par, t):
        return pltpu.make_async_remote_copy(
            src_ref=back.at[h, t],
            dst_ref=got_back.at[h, par, off],
            send_sem=back_send.at[h, t],
            recv_sem=back_recv.at[h, par, off],
            device_id=(at_row(row + off), t),
            device_id_type=MESH,
        )

    def ahead_copy(h, par, t):
        return pltpu.make_async_remote_copy(
            src_ref=ahead.at[h, t],
            dst_ref=got_ahead.at[h, par, off],
            send_sem=ahead_send.at[h, t],
            recv_sem=ahead_recv.at[h, par, off],
            device_id=(row, t),
            device_id_type=MESH,
        )

    def await_slot(ref, sem):
        pltpu.make_async_remote_copy(
            src_ref=ref, dst_ref=ref, send_sem=near_send.at[0, 0], recv_sem=sem,
            device_id=(row, lax.rem(off + 1, n_off)), device_id_type=MESH,
        ).wait_recv()

    def send_piece(h, par):
        for s in range(1, n_off):
            far_copy(h, par, s).start()
        for s in range(1, n_off):
            near_copy(h, par, s).start()

    def wait_back(h, par):
        @pl.when(off > 0)
        def _():
            for t in range(n_off):
                back_copy(h, par, t).wait_send()

    def wait_ahead(h, par):
        for s in range(1, n_off):
            ahead_copy(h, par, lax.rem(off + s, n_off)).wait_send()

    for h in range(CHAINS):
        send_piece(h, 0)
    load.wait()

    def dense_row(r, carry):
        for c in range(n_off):
            k = where_ref[r * n_off + c]
            block = jnp.where(k > 0, blocks[jnp.maximum(k - 1, 0)], 0.0)
            hi, lo = split(block)
            at = pl.ds(pl.multiple_of(r * bs, bs), bs)
            a_hi[at, c * bs:(c + 1) * bs] = hi
            a_lo[at, c * bs:(c + 1) * bs] = lo
            hi, lo = split(block.T)
            t_hi[c * bs:(c + 1) * bs, at] = hi
            t_lo[c * bs:(c + 1) * bs, at] = lo
        return carry

    lax.fori_loop(0, n_off, dense_row, 0)

    def put(t, x):
        hi = x.astype(jnp.bfloat16).astype(jnp.float32)
        lo = x - hi
        start = pl.multiple_of(t * bs, bs)
        xb[pl.ds(start, half), :] = jnp.where(left, hi, swap_halves(lo)).astype(jnp.bfloat16)
        xb[pl.ds(start + half, half), :] = jnp.where(left, swap_halves(hi), lo).astype(jnp.bfloat16)

    def product(hi_ref, lo_ref, at):
        both = jnp.dot(hi_ref[at, :], xb[...], preferred_element_type=jnp.float32)
        both += jnp.dot(lo_ref[at, :], xb[...], preferred_element_type=jnp.float32)
        return both + swap_halves(both)

    def packed(y, p):
        return jnp.where(left, y[p * bs:p * bs + half], y[p * bs + half:(p + 1) * bs])

    def multiply(h, par, k):
        put(off, cur[h, par])

        def take_near(s, carry):
            j = lax.rem(off + s, n_off)
            await_slot(near.at[h, par, j], near_recv.at[h, par, j])
            put(j, near[h, par, j])
            return carry

        lax.fori_loop(1, n_off, take_near, 0)

        @pl.when(k > 0)
        def _():
            wait_back(h, par)

        def back_chunk(i, carry):
            c = lax.rem(i + off // 2, n_chunks)
            at = pl.ds(pl.multiple_of(c * chunk, chunk), chunk)
            y = product(t_hi, t_lo, at)
            for p in range(per_chunk):
                t = c * per_chunk + p
                back[h, t] = packed(y, p)

                @pl.when(off > 0)
                def _():
                    back_copy(h, par, t).start()
            return carry

        lax.fori_loop(0, n_chunks, back_chunk, 0)

        @pl.when(off > 0)
        def _():
            def take_far(j, carry):
                await_slot(far.at[h, par, j], far_recv.at[h, par, j])
                put(j, far[h, par, j])
                return carry

            lax.fori_loop(0, n_off, take_far, 0)

        @pl.when(k > 0)
        def _():
            wait_ahead(h, par)

        def ahead_chunk(i, carry):
            c = lax.rem(i + off // 2 + 1, n_chunks)
            at = pl.ds(pl.multiple_of(c * chunk, chunk), chunk)
            y = product(a_hi, a_lo, at)
            for p in range(per_chunk):
                t = c * per_chunk + p
                ahead[h, t] = packed(y, p) + jnp.where(off == 0, back[h, t], 0.0)

                @pl.when(t != off)
                def _():
                    ahead_copy(h, par, t).start()
            return carry

        lax.fori_loop(0, n_chunks, ahead_chunk, 0)

    def collect(h, par, k):
        total = ahead[h, off]
        for s in range(1, n_off):
            j = lax.rem(off + s, n_off)
            await_slot(got_ahead.at[h, par, j], ahead_recv.at[h, par, j])
            total += got_ahead[h, par, j]
        for s in range(1, n_off):
            await_slot(got_back.at[h, par, s], back_recv.at[h, par, s])
            total += got_back[h, par, s]
        scale = jnp.where(k == 0, first_scale, later_scale)
        nxt = lax.rem(k + 1, 2)
        cur[h, nxt] = scale * total - cur[h, nxt]
        for s in range(1, n_off):
            near_copy(h, par, s).wait_send()
            far_copy(h, par, s).wait_send()

        @pl.when(k < DEGREE - 1)
        def _():
            send_piece(h, nxt)

    def step(k, carry):
        par = lax.rem(k, 2)

        def each(what):
            def one(h, carry):
                what(h, par, k)
                return carry

            lax.fori_loop(0, CHAINS, one, 0)

        each(multiply)
        each(collect)
        return carry

    lax.fori_loop(0, DEGREE, step, 0)
    last = DEGREE % 2
    for h in range(CHAINS):
        wait_back(h, 1 - last)
        wait_ahead(h, 1 - last)
    out_ref[:half, :] = jnp.where(left, cur[0, last], swap_halves(cur[1, last]))
    out_ref[half:, :] = jnp.where(left, swap_halves(cur[0, last]), cur[1, last])


def solution(mesh):
    n_row, n_off = mesh.shape["row"], mesh.shape["off"]

    def per_device(vectors, blocks, lists):
        bs, width = vectors.shape
        rows = n_off * bs
        half = bs // 2
        count = blocks.shape[2]
        position = lists[0, 0, 0] * n_off + lists[0, 0, 1]
        hit = position[None, :] == jnp.arange(n_off * n_off, dtype=jnp.int32)[:, None]
        where = jnp.sum(
            jnp.where(hit, jnp.arange(1, count + 1, dtype=jnp.int32)[None, :], 0),
            axis=1, dtype=jnp.int32,
        )
        f32, bf16 = jnp.float32, jnp.bfloat16
        dma = pltpu.SemaphoreType.DMA
        slots = pltpu.VMEM((CHAINS, 2, n_off, half, width), f32)
        staged = pltpu.VMEM((CHAINS, n_off, half, width), f32)
        return pl.pallas_call(
            functools.partial(kernel, n_row, n_off, bs, 2 * bs),
            out_shape=jax.ShapeDtypeStruct((bs, width), f32),
            in_specs=[
                pl.BlockSpec(memory_space=pltpu.SMEM),
                pl.BlockSpec(memory_space=pltpu.VMEM),
                pl.BlockSpec(memory_space=pl.ANY),
            ],
            out_specs=pl.BlockSpec(memory_space=pltpu.VMEM),
            scratch_shapes=[
                pltpu.VMEM((count, bs, bs), f32),
                pltpu.VMEM((rows, rows), bf16),
                pltpu.VMEM((rows, rows), bf16),
                pltpu.VMEM((rows, rows), bf16),
                pltpu.VMEM((rows, rows), bf16),
                pltpu.VMEM((CHAINS, 2, half, width), f32),
                slots,
                slots,
                pltpu.VMEM((rows, width), bf16),
                staged,
                staged,
                slots,
                slots,
                dma,
                dma((CHAINS, n_off)),
                dma((CHAINS, n_off)),
                dma((CHAINS, 2, n_off)),
                dma((CHAINS, 2, n_off)),
                dma((CHAINS, n_off)),
                dma((CHAINS, n_off)),
                dma((CHAINS, 2, n_off)),
                dma((CHAINS, 2, n_off)),
            ],
            compiler_params=pltpu.CompilerParams(collective_id=0, has_side_effects=True),
        )(where, vectors, blocks[0, 0])

    return jax.shard_map(
        per_device,
        mesh=mesh,
        in_specs=(
            P(("row", "off"), None),
            P("row", "off", None, None, None),
            P("row", "off", None, None),
        ),
        out_specs=P(("row", "off"), None),
        check_vma=False,
    )
```

```python
import functools

import jax
import jax.numpy as jnp
from jax import lax
from jax.experimental import pallas as pl
from jax.experimental.pallas import tpu as pltpu
from jax.sharding import PartitionSpec as P

DEGREE = 4
CHAINS = 2
MESH = pl.DeviceIdType.MESH

first_scale = 0.4
later_scale = 0.8


def split(x):
    hi = x.astype(jnp.bfloat16)
    lo = (x - hi.astype(jnp.float32)).astype(jnp.bfloat16)
    return hi, lo


def swap_halves(x):
    return pltpu.roll(x, x.shape[1] // 2, 1)


def left_of(shape):
    return lax.broadcasted_iota(jnp.int32, shape, 1) < shape[1] // 2


def kernel(
    n_row, n_off, bs, chunk,
    where_ref, vec_ref, blocks_hbm, out_ref,
    blocks, a_hi, a_lo, t_hi, t_lo, cur, near, far, xb, ahead, back, got_ahead, got_back,
    load_sem, near_send, far_send, near_recv, far_recv, ahead_send, back_send, ahead_recv, back_recv,
):
    row = lax.axis_index("row")
    off = lax.axis_index("off")
    rows = n_off * bs
    half = bs // 2
    per_chunk = chunk // bs
    n_chunks = rows // chunk
    left = left_of((half, bs))

    def at_row(r):
        return lax.rem(r + n_row, n_row)

    load = pltpu.make_async_copy(blocks_hbm, blocks, load_sem)
    load.start()

    barrier = pltpu.get_barrier_semaphore()
    for s in range(1, n_off):
        pl.semaphore_signal(
            barrier, inc=1, device_id=(row, lax.rem(off + s, n_off)), device_id_type=MESH
        )
        pl.semaphore_signal(barrier, inc=1, device_id=(at_row(row - s), s), device_id_type=MESH)

    @pl.when(off > 0)
    def _():
        for t in range(n_off):
            pl.semaphore_signal(
                barrier, inc=1, device_id=(at_row(row + off), t), device_id_type=MESH
            )

    upper, lower = vec_ref[:half, :], vec_ref[half:, :]
    cur[0, 0] = jnp.where(left, upper, swap_halves(lower))
    cur[1, 0] = jnp.where(left, swap_halves(upper), lower)
    for h in range(CHAINS):
        cur[h, 1] = jnp.zeros((half, bs), jnp.float32)

    @pl.when(off > 0)
    def _():
        pl.semaphore_wait(barrier, 3 * n_off - 2)

    @pl.when(off == 0)
    def _():
        pl.semaphore_wait(barrier, 2 * n_off - 2)

    def near_copy(h, par, s):
        return pltpu.make_async_remote_copy(
            src_ref=cur.at[h, par],
            dst_ref=near.at[h, par, off],
            send_sem=near_send.at[h, s],
            recv_sem=near_recv.at[h, par, off],
            device_id=(row, lax.rem(off + s, n_off)),
            device_id_type=MESH,
        )

    def far_copy(h, par, s):
        d = 1 + lax.rem(s + off, n_off - 1)
        return pltpu.make_async_remote_copy(
            src_ref=cur.at[h, par],
            dst_ref=far.at[h, par, off],
            send_sem=far_send.at[h, s],
            recv_sem=far_recv.at[h, par, off],
            device_id=(at_row(row - d), d),
            device_id_type=MESH,
        )

    def back_copy(h, par, t):
        return pltpu.make_async_remote_copy(
            src_ref=back.at[h, t],
            dst_ref=got_back.at[h, par, off],
            send_sem=back_send.at[h, t],
            recv_sem=back_recv.at[h, par, off],
            device_id=(at_row(row + off), t),
            device_id_type=MESH,
        )

    def ahead_copy(h, par, t):
        return pltpu.make_async_remote_copy(
            src_ref=ahead.at[h, t],
            dst_ref=got_ahead.at[h, par, off],
            send_sem=ahead_send.at[h, t],
            recv_sem=ahead_recv.at[h, par, off],
            device_id=(row, t),
            device_id_type=MESH,
        )

    def await_slot(ref, sem):
        pltpu.make_async_remote_copy(
            src_ref=ref, dst_ref=ref, send_sem=near_send.at[0, 0], recv_sem=sem,
            device_id=(row, lax.rem(off + 1, n_off)), device_id_type=MESH,
        ).wait_recv()

    def send_piece(h, par):
        for s in range(1, n_off):
            near_copy(h, par, s).start()
        for s in range(1, n_off):
            far_copy(h, par, s).start()

    def wait_back(h, par):
        @pl.when(off > 0)
        def _():
            for t in range(n_off):
                back_copy(h, par, t).wait_send()

    def wait_ahead(h, par):
        for s in range(1, n_off):
            ahead_copy(h, par, lax.rem(off + s, n_off)).wait_send()

    for h in range(CHAINS):
        send_piece(h, 0)
    load.wait()

    def dense_row(r, carry):
        for c in range(n_off):
            k = where_ref[r * n_off + c]
            block = jnp.where(k > 0, blocks[jnp.maximum(k - 1, 0)], 0.0)
            hi, lo = split(block)
            at = pl.ds(pl.multiple_of(r * bs, bs), bs)
            a_hi[at, c * bs:(c + 1) * bs] = hi
            a_lo[at, c * bs:(c + 1) * bs] = lo
            hi, lo = split(block.T)
            t_hi[c * bs:(c + 1) * bs, at] = hi
            t_lo[c * bs:(c + 1) * bs, at] = lo
        return carry

    lax.fori_loop(0, n_off, dense_row, 0)

    def put(t, x):
        hi = x.astype(jnp.bfloat16).astype(jnp.float32)
        lo = x - hi
        start = pl.multiple_of(t * bs, bs)
        xb[pl.ds(start, half), :] = jnp.where(left, hi, swap_halves(lo)).astype(jnp.bfloat16)
        xb[pl.ds(start + half, half), :] = jnp.where(left, swap_halves(hi), lo).astype(jnp.bfloat16)

    def product(hi_ref, lo_ref, at):
        both = jnp.dot(hi_ref[at, :], xb[...], preferred_element_type=jnp.float32)
        both += jnp.dot(lo_ref[at, :], xb[...], preferred_element_type=jnp.float32)
        return both + swap_halves(both)

    def packed(y, p):
        return jnp.where(left, y[p * bs:p * bs + half], y[p * bs + half:(p + 1) * bs])

    def multiply(h, par, k):
        put(off, cur[h, par])

        def take_near(s, carry):
            j = lax.rem(off + s, n_off)
            await_slot(near.at[h, par, j], near_recv.at[h, par, j])
            put(j, near[h, par, j])
            return carry

        lax.fori_loop(1, n_off, take_near, 0)

        @pl.when(k > 0)
        def _():
            wait_back(h, par)

        def back_chunk(i, carry):
            c = lax.rem(i + off // 2, n_chunks)
            at = pl.ds(pl.multiple_of(c * chunk, chunk), chunk)
            y = product(t_hi, t_lo, at)
            for p in range(per_chunk):
                t = c * per_chunk + p
                back[h, t] = packed(y, p)

                @pl.when(off > 0)
                def _():
                    back_copy(h, par, t).start()
            return carry

        lax.fori_loop(0, n_chunks, back_chunk, 0)

        @pl.when(off > 0)
        def _():
            def take_far(j, carry):
                await_slot(far.at[h, par, j], far_recv.at[h, par, j])
                put(j, far[h, par, j])
                return carry

            lax.fori_loop(0, n_off, take_far, 0)

        @pl.when(k > 0)
        def _():
            wait_ahead(h, par)

        def ahead_chunk(i, carry):
            c = lax.rem(i + off // 2 + 1, n_chunks)
            at = pl.ds(pl.multiple_of(c * chunk, chunk), chunk)
            y = product(a_hi, a_lo, at)
            for p in range(per_chunk):
                t = c * per_chunk + p
                ahead[h, t] = packed(y, p) + jnp.where(off == 0, back[h, t], 0.0)

                @pl.when(t != off)
                def _():
                    ahead_copy(h, par, t).start()
            return carry

        lax.fori_loop(0, n_chunks, ahead_chunk, 0)

    def collect(h, par, k):
        total = ahead[h, off]
        for s in range(1, n_off):
            j = lax.rem(off + s, n_off)
            await_slot(got_ahead.at[h, par, j], ahead_recv.at[h, par, j])
            total += got_ahead[h, par, j]
        for s in range(1, n_off):
            await_slot(got_back.at[h, par, s], back_recv.at[h, par, s])
            total += got_back[h, par, s]
        scale = jnp.where(k == 0, first_scale, later_scale)
        nxt = lax.rem(k + 1, 2)
        cur[h, nxt] = scale * total - cur[h, nxt]
        for s in range(1, n_off):
            near_copy(h, par, s).wait_send()
            far_copy(h, par, s).wait_send()

        @pl.when(k < DEGREE - 1)
        def _():
            send_piece(h, nxt)

    def step(k, carry):
        par = lax.rem(k, 2)

        def each(what):
            def one(h, carry):
                what(h, par, k)
                return carry

            lax.fori_loop(0, CHAINS, one, 0)

        each(multiply)
        each(collect)
        return carry

    lax.fori_loop(0, DEGREE, step, 0)
    last = DEGREE % 2
    for h in range(CHAINS):
        wait_back(h, 1 - last)
        wait_ahead(h, 1 - last)
    out_ref[:half, :] = jnp.where(left, cur[0, last], swap_halves(cur[1, last]))
    out_ref[half:, :] = jnp.where(left, swap_halves(cur[0, last]), cur[1, last])


def solution(mesh):
    n_row, n_off = mesh.shape["row"], mesh.shape["off"]

    def per_device(vectors, blocks, lists):
        bs, width = vectors.shape
        rows = n_off * bs
        half = bs // 2
        count = blocks.shape[2]
        position = lists[0, 0, 0] * n_off + lists[0, 0, 1]
        hit = position[None, :] == jnp.arange(n_off * n_off, dtype=jnp.int32)[:, None]
        where = jnp.sum(
            jnp.where(hit, jnp.arange(1, count + 1, dtype=jnp.int32)[None, :], 0),
            axis=1, dtype=jnp.int32,
        )
        f32, bf16 = jnp.float32, jnp.bfloat16
        dma = pltpu.SemaphoreType.DMA
        slots = pltpu.VMEM((CHAINS, 2, n_off, half, width), f32)
        staged = pltpu.VMEM((CHAINS, n_off, half, width), f32)
        return pl.pallas_call(
            functools.partial(kernel, n_row, n_off, bs, 2 * bs),
            out_shape=jax.ShapeDtypeStruct((bs, width), f32),
            in_specs=[
                pl.BlockSpec(memory_space=pltpu.SMEM),
                pl.BlockSpec(memory_space=pltpu.VMEM),
                pl.BlockSpec(memory_space=pl.ANY),
            ],
            out_specs=pl.BlockSpec(memory_space=pltpu.VMEM),
            scratch_shapes=[
                pltpu.VMEM((count, bs, bs), f32),
                pltpu.VMEM((rows, rows), bf16),
                pltpu.VMEM((rows, rows), bf16),
                pltpu.VMEM((rows, rows), bf16),
                pltpu.VMEM((rows, rows), bf16),
                pltpu.VMEM((CHAINS, 2, half, width), f32),
                slots,
                slots,
                pltpu.VMEM((rows, width), bf16),
                staged,
                staged,
                slots,
                slots,
                dma,
                dma((CHAINS, n_off)),
                dma((CHAINS, n_off)),
                dma((CHAINS, 2, n_off)),
                dma((CHAINS, 2, n_off)),
                dma((CHAINS, n_off)),
                dma((CHAINS, n_off)),
                dma((CHAINS, 2, n_off)),
                dma((CHAINS, 2, n_off)),
            ],
            compiler_params=pltpu.CompilerParams(collective_id=0, has_side_effects=True),
        )(where, vectors, blocks[0, 0])

    return jax.shard_map(
        per_device,
        mesh=mesh,
        in_specs=(
            P(("row", "off"), None),
            P("row", "off", None, None, None),
            P("row", "off", None, None),
        ),
        out_specs=P(("row", "off"), None),
        check_vma=False,
    )
```
